256 devices in a mesh: row: 16 (over z, core), col: 16 (over y, x).
Axes of the slice: x: 4, y: 4, z: 8, core: 2. Of those that a mesh axis runs over, the one named last changes fastest.
Arguments:
- factor: float32 [2, 16, 512, 2, 16, 512], P(None, 'row', None, None, 'col'), as said below
- pending: float32 [2, 16, 512, 16384], P(None, 'row', None, 'col'), may hold values from -0.4 to 0.4
- variance: float32 [16384], P('col'), may hold values from 2 to 4
- first_block: int32 [1], replicated, may hold values from 0 to 30
Outputs:
- pending_out: float32 [2, 16, 512, 16384], P(None, 'row', None, 'col')
- variance_out: float32 [16384], P('col')
The draws below stay inside these ranges and needn't reach their ends.
Inputs may be any that keep to these rules, and one draw needn't show every extreme that they name: factor is lower triangular with diagonal entries from 1 to 2.
All inputs are finite; a program needn't handle non-finite values.
Results may differ from the reference program's by a relative error of at most 0.0001.
Values sent between devices are 32-bit elements; how exact they have to be, the bound alone decides.
A program may use at most 128 MiB of HBM per device.

```python
import math
import jax
import jax.numpy as jnp
from jax import lax

N = 16384
B = 512
NB = 32
RCYC = 2
CCYC = 2
Q = 16384
N_ROW = 16


def draw_factor(key, part):
    nrow = NB // RCYC
    ncol = NB // CCYC
    shape = (RCYC, nrow, B, CCYC, ncol, B)
    key_diag = jax.random.fold_in(key, 11)
    key_inner = jax.random.fold_in(key, 12)
    key_dense = jax.random.fold_in(key, 13)
    cyc_row = lax.broadcasted_iota(jnp.int32, shape, 0)
    dev_row = lax.broadcasted_iota(jnp.int32, shape, 1)
    in_row = lax.broadcasted_iota(jnp.int32, shape, 2)
    cyc_col = lax.broadcasted_iota(jnp.int32, shape, 3)
    dev_col = lax.broadcasted_iota(jnp.int32, shape, 4)
    in_col = lax.broadcasted_iota(jnp.int32, shape, 5)
    block_row = cyc_row * nrow + dev_row
    block_col = cyc_col * ncol + dev_col
    glob_row = block_row * B + in_row
    glob_col = block_col * B + in_col
    diag_vals = jax.random.uniform(key_diag, shape, jnp.float32, 1.0, 2.0)
    distance = jnp.maximum(glob_row - glob_col - 1, 0).astype(jnp.float32)
    falloff = jnp.exp(distance * jnp.float32(math.log(0.6)))
    inner_vals = jax.random.uniform(key_inner, shape, jnp.float32, 0.2, 1.0) * falloff * jnp.float32(0.9 * 0.4)
    dense_vals = jax.random.normal(key_dense, shape, jnp.float32) * (0.7 / math.sqrt(B))
    value = jnp.where(block_row > block_col, dense_vals, jnp.float32(0.0))
    value = jnp.where((block_row == block_col) & (glob_row > glob_col), inner_vals, value)
    value = jnp.where(glob_row == glob_col, diag_vals, value)
    return value.astype(jnp.float32)


def level_of(rng, shape, pieces, low, top_value):
    factor_of, own = 1.0, jax.random.fold_in(rng, 6)
    for position, blocks in pieces:
        draws = jnp.exp(jax.random.uniform(jax.random.fold_in(own, position), (blocks,), jnp.float32, low / len(pieces), top_value / len(pieces)))
        factor_of = factor_of * jnp.repeat(draws, shape[position] // blocks).reshape([-1 if axis == position else 1 for axis in range(len(shape))])
    return factor_of


def bell_draw(stream_key, dims, deviation, most, split=(), held_as=jnp.bfloat16):
    factor_of = level_of(stream_key, dims, split, -0.22, 0.18) if split else 1.0
    drawn = jax.random.normal(stream_key, dims, jnp.float32) * deviation * factor_of
    return jnp.minimum(jnp.maximum(drawn, -most), most).astype(held_as)


def setup_inputs(seed: int = 0) -> dict:
    seeds = jax.random.split(jax.random.key(seed), 5)
    factor = draw_factor(jax.random.fold_in(seeds[4], 71), 0)
    pending = bell_draw(seeds[1], (RCYC, N_ROW, B, Q), 0.05, 0.4, ((1, 16), (3, 16)), jnp.float32)
    variance = jnp.clip(2.0 + 2.0 * jax.random.uniform(seeds[2], (Q,), jnp.float32) ** level_of(seeds[2], (Q,), ((0, 16),), -0.2, 0.2), 2.0, 4.0)
    first_block = jax.random.randint(seeds[3], (1,), 0, NB - 1).astype(jnp.int32)
    return dict(factor=factor, pending=pending, variance=variance, first_block=first_block)


def reference(factor, pending, variance, first_block):
    lower = factor.reshape(N, N)
    work = pending.reshape(N, Q)
    first = first_block[0].astype(jnp.int32)
    block_of_row = (jnp.arange(N, dtype=jnp.int32) // B).astype(jnp.int32)
    zero = jnp.zeros((), jnp.int32)
    for offset in range(2):
        index = (first + offset).astype(jnp.int32)
        start = (index * B).astype(jnp.int32)
        diagonal = lax.dynamic_slice(lower, (start, start), (B, B))
        rows_now = lax.dynamic_slice(work, (start, zero), (B, Q))
        solved = jax.scipy.linalg.solve_triangular(diagonal, rows_now, lower=True)
        panel_cols = lax.dynamic_slice(lower, (zero, start), (N, B))
        product = jnp.dot(panel_cols.astype(jnp.float32), solved.astype(jnp.float32), precision=lax.Precision.HIGHEST, preferred_element_type=jnp.float32)
        work = jnp.where((block_of_row > index)[:, None], work - product, work)
        work = lax.dynamic_update_slice(work, solved, (start, zero))
        variance = variance - jnp.sum(solved * solved, axis=0)
    return (work.reshape(pending.shape), variance)
```

```python
import functools

import jax
import jax.numpy as jnp
import numpy as np
from jax import lax
from jax.experimental import pallas as pl
from jax.experimental.pallas import tpu as pltpu
from jax.sharding import PartitionSpec as P

MESH = pl.DeviceIdType.MESH
F32 = jnp.float32
BF16 = jnp.bfloat16

PI = [
    [-1, 0, 0, 0, 1, 2, 2, 0, 1, 2, 2, 0, 1, 3, 0, 0],
    [-1, 1, 1, 1, 0, 1, 1, 2, 0, 1, 3, 2, 0, 1, 3, 3],
    [-1, 3, 3, 3, 2, 0, 0, 1, 2, 0, 1, 1, 2, 2, 2, 2],
    [-1, 2, 2, 2, 3, 3, 3, 3, 3, 3, 0, 3, 3, 0, 1, 1],
]
K = [
    [0, 1, 2, 3, 3, 2, 3, 4, 4, 3, 4, 5, 3, 2, 3, 4],
    [0, 3, 2, 1, 3, 4, 3, 2, 4, 5, 4, 3, 3, 4, 3, 2],
    [0, 3, 4, 3, 1, 2, 3, 2, 2, 3, 4, 3, 3, 4, 5, 4],
    [0, 3, 4, 3, 3, 4, 5, 4, 2, 3, 4, 3, 1, 2, 3, 2],
]
STEP = [(1, 0), (3, 0), (0, 1), (0, 3)]
DEPTH = 5
D = 4
NP = 32
SXY = NP + (DEPTH - 1) * D
SZ = NP + 7 * D
ZSEND = NP + 6 * D
EV_A2A, EV_SEL, EV_AG = 12, 20, 28
EV_STEP = 4


def hop(v, d):
    return ((v // 4 + STEP[d][1]) % 4) * 4 + (v % 4 + STEP[d][0]) % 4


def tree_table():
    rows = []
    for u in range(16):
        pick = []
        for d in range(4):
            v = hop(u, d)
            if u == 0 or v == 0:
                pick.append(4)
            else:
                c = [c for c in range(4) if PI[c][v] == d][0]
                pick.append(PI[c][u])
        rows.append(pick + [max(PI[c][u], 0) for c in range(4)] + [max(K[c][u] - 1, 0) * D for c in range(4)])
    return np.array(rows, np.int32).reshape(-1)


def iota2(n, dim):
    return lax.broadcasted_iota(jnp.int32, (n, n), dim)


def dot6(a, b):
    return jnp.dot(a, b, precision=lax.Precision.HIGHEST, preferred_element_type=F32)


def split(x):
    hi = x.astype(BF16)
    return hi, (x - hi.astype(F32)).astype(BF16)


def dot3(ah, al, bh, bl):
    f = functools.partial(jnp.dot, preferred_element_type=F32)
    return f(ah, bh) + (f(ah, bl) + f(al, bh))


def inverses(blocks):
    n = blocks[0].shape[0]
    r, c = iota2(n, 0), iota2(n, 1)
    eye = (r == c).astype(F32)
    scale = [1.0 / jnp.sum(jnp.where(r == c, b, 0.0), axis=1, keepdims=True) for b in blocks]
    scale_t = [1.0 / jnp.sum(jnp.where(r == c, b, 0.0), axis=0, keepdims=True) for b in blocks]
    strict = [jnp.where(r > c, b * s, 0.0) for b, s in zip(blocks, scale)]
    small = [jnp.where(r // 16 == c // 16, x, 0.0) for x in strict]
    inv = [eye - x for x in small]
    power = small
    for _ in range(3):
        power = [dot6(x, x) for x in power]
        inv = [dot6(e, eye + x) for e, x in zip(inv, power)]
    size = 16
    while size < n:
        off = [jnp.where((r // (2 * size) == c // (2 * size)) & (r // size != c // size), x, 0.0) for x in strict]
        mid = [dot6(f, e) for f, e in zip(off, inv)]
        inv = [e - dot6(e, m) for e, m in zip(inv, mid)]
        size *= 2
    return [e * s for e, s in zip(inv, scale_t)]


def exchange(
    first_ref, tbl_ref, f_ref, w_ref, var_ref,
    xh_ref, xl_ref, ph_ref, pl_ref, varo_ref,
    xst, xrc, zst, zrc, zpt, cand, ta, tb, tab, a2a, tg, lh, ll, dh, dl,
    xs, xr, zs, zr, zps, zpr, scs, scr, a2s, a2r, ags, agr, x2s, x2r, tps, tpr,
):
    p = lax.axis_index("row")
    s = lax.axis_index("col")
    zc, core = p // 2, lax.rem(p, 2)
    yc, xc = s // 4, lax.rem(s, 4)
    partner = (p + 1 - 2 * core, s)
    near = [
        (p, yc * 4 + lax.rem(xc + 1, 4)),
        (p, yc * 4 + lax.rem(xc + 3, 4)),
        (p, lax.rem(yc + 1, 4) * 4 + xc),
        (p, lax.rem(yc + 3, 4) * 4 + xc),
    ]
    zup = (lax.rem(zc + 1, 8) * 2 + core, s)
    zdn = (lax.rem(zc + 7, 8) * 2 + core, s)
    znear = [zup, zdn]

    def rcopy(src, dst, ssem, rsem, dev):
        return pltpu.make_async_remote_copy(
            src_ref=src, dst_ref=dst, send_sem=ssem, recv_sem=rsem, device_id=dev, device_id_type=MESH
        )

    barrier = pltpu.get_barrier_semaphore()
    for o in range(1, 16):
        pl.semaphore_signal(barrier, inc=1, device_id=(p, lax.rem(s + o, 16)), device_id_type=MESH)
        pl.semaphore_signal(barrier, inc=1, device_id=(lax.rem(p + o, 16), s), device_id_type=MESH)

    j = first_ref[0]
    j1 = j + 1
    pj, pj1 = lax.rem(j, 16), lax.rem(j1, 16)
    c1, c2 = j // 16, j1 // 16
    crit = jnp.where(p == pj1, c2, c1)
    zroot = (p == pj) | (p == pj1)
    rel = []
    for root in (pj, pj1):
        ry, rx = root // 4, lax.rem(root, 4)
        rel.append((lax.rem(yc - ry + 4, 4) * 4 + lax.rem(xc - rx + 4, 4)) * 12)
    pick = [[tbl_ref[rel[q] + d] for d in range(4)] for q in range(2)]
    where_dir = [[tbl_ref[rel[q] + 4 + c] for c in range(4)] for q in range(2)]
    where_slot = [[tbl_ref[rel[q] + 8 + c] for c in range(4)] for q in range(2)]
    proot = [rel[0] == 0, rel[1] == 0]
    cyc = [c1, c2]

    def panel(row, cyc_q, ct):
        low, high = (f_ref[pl.ds(row * 8 + c * 4 + ct, 8, stride=8), :] for c in range(2))
        return jnp.where(cyc_q == 0, low, high)

    def rhs(row):
        low, high = (w_ref[pl.ds(pl.multiple_of(a * 512 + row, 8), 8), :] for a in range(2))
        return jnp.where(crit == 0, low, high)

    is_a = s == p
    is_b = s == lax.rem(p + 15, 16)
    cidx = jnp.where(is_a, crit, c1)

    @pl.when(is_a | is_b)
    def _():
        def fill(q, _):
            for u in range(16):
                low, high = (panel(a * 512 + q * 32 + (u // 4) * 8, cidx, u % 4) for a in range(2))
                cand[q, u] = jnp.where(crit == 0, low, high)
            return 0

        lax.fori_loop(0, 16, fill, 0)

    pl.semaphore_wait(barrier, 30)

    for flag, dest, k in ((is_a, ta, 0), (is_b, tb, 1)):

        @pl.when(flag)
        def _():
            for o in range(1, 16):
                to = lax.rem(s + o, 16)
                rcopy(cand.at[to], dest, scs, scr.at[k], (p, to)).start()

    def ev_a2a():
        for flag, dest, k in ((is_a, ta, 0), (is_b, tb, 1)):

            @pl.when(flag)
            def _():
                for u in range(16):
                    dest[u] = cand[s, u]

            @pl.when(jnp.logical_not(flag))
            def _():
                rcopy(cand.at[0], dest, scs, scr.at[k], partner).wait_recv()

        for u in range(16):
            tab[u, 0] = ta[u]
            tab[u, 1] = tb[u]
        a2a[p] = tab[p]
        for o in range(1, 16):
            to = lax.rem(p + o, 16)
            rcopy(tab.at[to], a2a.at[p], a2s, a2r.at[p], (to, s)).start()

    def ev_sel():
        for o in range(1, 16):
            frm = lax.rem(p + o, 16)
            rcopy(tab.at[0], a2a.at[frm], a2s, a2r.at[frm], partner).wait_recv()
        h, u = p // 8, lax.rem(p, 8)
        tg[h, s, u, 0] = a2a[pj, 0]
        tg[h, s, u, 1] = a2a[pj1, 0]
        tg[h, s, u, 2] = a2a[pj1, 1]
        for o in range(1, 16):
            to = lax.rem(p + o, 16)
            rcopy(tg.at[h, s, u], tg.at[h, s, u], ags, agr.at[p], (to, s)).start()

    def piece(root, c):
        return tg.at[core, root, pl.ds(2 * c, 2)]

    def ev_ag(k):
        if k == 0:
            for o in range(1, 16):
                frm = lax.rem(p + o, 16)
                rcopy(
                    tg.at[0, 0, 0], tg.at[frm // 8, s, lax.rem(frm, 8)], ags, agr.at[frm], partner
                ).wait_recv()
        for w in range(16):
            for c in range(4):
                if K[c][w] != k:
                    continue
                root = lax.rem(yc + 4 - w // 4, 4) * 4 + lax.rem(xc + 4 - w % 4, 4)
                if w:
                    rcopy(piece(root, c), piece(root, c), x2s, x2r.at[root, c], partner).wait_recv()
                    rcopy(piece(root, c), piece(root, c), tps, tpr, partner).start()
                for d in range(4):
                    v = hop(w, d)
                    if v and PI[c][v] == d and (w or d == c):
                        rcopy(piece(root, c), piece(root, c), x2s, x2r.at[root, c], near[d]).start()

    def slot(t, _):
        i = jnp.minimum(t, NP - 1)
        back = t - D

        @pl.when((t >= D) & (back < SXY))
        def _():
            for d in range(4):
                rcopy(xst.at[d, back], xrc.at[d, back], xs.at[d], xr.at[d, back], near[d]).wait_recv()

        @pl.when((t >= D) & (back < ZSEND))
        def _():
            for d in range(2):
                rcopy(zst.at[d, back], zrc.at[d, back], zs.at[d], zr.at[d, back], znear[d]).wait_recv()

        @pl.when(t < D)
        def _():
            for d in range(4):
                for q in range(2):
                    for ct in range(4):
                        xst[d, t, q, :, ct * 128 : ct * 128 + 128] = panel(d * 256 + i * 8, cyc[q], ct)
            for d in range(2):
                zst[d, t] = rhs(d * 256 + i * 8)

        @pl.when((t >= D) & (t < SXY))
        def _():
            for d in range(4):
                for q in range(2):
                    for ct in range(4):
                        lanes = slice(ct * 128, ct * 128 + 128)
                        v = panel(d * 256 + i * 8, cyc[q], ct)
                        for e in range(4):
                            v = jnp.where(pick[q][d] == e, xrc[e, back, q, :, lanes], v)
                        xst[d, t, q, :, lanes] = v

        @pl.when(t >= D)
        def _():
            for d in range(2):
                zst[d, t] = jnp.where(zroot, rhs(d * 256 + i * 8), zrc[d, jnp.minimum(back, ZSEND - 1)])

        @pl.when(t < SXY)
        def _():
            for d in range(4):
                rcopy(xst.at[d, t], xrc.at[d, t], xs.at[d], xr.at[d, t], near[d]).start()

        @pl.when(t < ZSEND)
        def _():
            for d in range(2):
                rcopy(zst.at[d, t], zrc.at[d, t], zs.at[d], zr.at[d, t], znear[d]).start()

        for d in range(2):
            rcopy(zst.at[d, t], zpt.at[d, t], zps.at[d], zpr.at[d], partner).start()

        pl.when(t == EV_A2A)(ev_a2a)
        pl.when(t == EV_SEL)(ev_sel)
        for k in range(DEPTH + 1):
            pl.when(t == EV_AG + k * EV_STEP)(functools.partial(ev_ag, k))
        return 0

    lax.fori_loop(0, SZ, slot, 0)

    for d in range(4):
        rcopy(xst.at[d], xrc.at[d], xs.at[d], xr.at[d, 0], partner).wait_send()
    for d in range(2):
        rcopy(zrc.at[d], zrc.at[d], zs.at[d], zr.at[d, 0], partner).wait_send()
        rcopy(zst.at[d], zpt.at[d], zps.at[d], zpr.at[d], partner).wait()
    half = tg.at[core, pl.ds(0, 15)]
    rcopy(half, half, x2s, tpr, partner).wait_send()
    rcopy(half, half, tps, tpr, partner).wait()
    rcopy(a2a.at[pl.ds(0, 15)], a2a.at[pl.ds(0, 15)], a2s, tpr, partner).wait_send()
    rcopy(tg.at[0, pl.ds(0, 15), 0], tg.at[0, pl.ds(0, 15), 0], ags, tpr, partner).wait_send()

    @pl.when(is_a | is_b)
    def _():
        rcopy(cand.at[pl.ds(0, 15)], cand.at[pl.ds(0, 15)], scs, tpr, partner).wait_send()

    def panels(g, colour, i):
        for q in range(2):
            for ct in range(4):
                parts = []
                for e in range(2):
                    got = xrc[where_dir[q][colour], i + e + where_slot[q][colour], q, :, ct * 128 : ct * 128 + 128]
                    own = panel(g * 16 + e * 8, cyc[q], ct)
                    parts.append(jnp.where(proot[q], own, got))
                hi, lo = split(jnp.concatenate(parts, axis=0))
                lanes = slice(q * 512 + ct * 128, q * 512 + ct * 128 + 128)
                ph_ref[pl.ds(pl.multiple_of(g * 16, 16), 16), lanes] = hi
                pl_ref[pl.ds(pl.multiple_of(g * 16, 16), 16), lanes] = lo

    for colour in range(4):

        def rows(n, _):
            panels(colour * 16 + n, colour, n * 2)
            return 0

        lax.fori_loop(0, 16, rows, 0)

    def tile(b, rt, ct):
        u = (rt % 4) * 4 + ct
        return tg[u // 8, rt // 4, u % 8, b]

    def triangle(q, _):
        for b in range(3):
            for pair in range(2):
                for ct in range(4):
                    u = pair * 8 + ct
                    x = jnp.concatenate([tg[u // 8, q, u % 8, b], tg[(u + 4) // 8, q, (u + 4) % 8, b]], axis=0)
                    hi, lo = split(x)
                    rows16 = pl.ds(pl.multiple_of(q * 32 + pair * 16, 16), 16)
                    lh[b, rows16, ct * 128 : ct * 128 + 128] = hi
                    ll[b, rows16, ct * 128 : ct * 128 + 128] = lo
        return 0

    lax.fori_loop(0, 16, triangle, 0)

    def square(b, m, k):
        return jnp.concatenate(
            [
                jnp.concatenate([tile(b, m * 16 + rt, k * 1 + ct) for ct in range(1)], axis=1)
                for rt in range(16)
            ],
            axis=0,
        )

    inv = inverses([square(b, m, m) for b in range(2) for m in range(4)])
    for b in range(2):
        for m in range(2):
            top, bottom = inv[b * 4 + 2 * m], inv[b * 4 + 2 * m + 1]
            corner = -dot6(bottom, dot6(square(b, 2 * m + 1, 2 * m), top))
            for (r0, c0), x in (((0, 0), top), ((1, 1), bottom), ((1, 0), corner), ((0, 1), jnp.zeros_like(top))):
                hi, lo = split(x)
                dh[b * 2 + m, r0 * 128 : r0 * 128 + 128, c0 * 128 : c0 * 128 + 128] = hi
                dl[b * 2 + m, r0 * 128 : r0 * 128 + 128, c0 * 128 : c0 * 128 + 128] = lo

    zroots = [pj // 2, pj1 // 2]
    source = [lax.rem(pj, 2) == core, lax.rem(pj1, 2) == core]
    late = [
        [lax.rem(zc - z + 8, 8) * D for z in zroots],
        [lax.rem(z - zc + 8, 8) * D for z in zroots],
    ]

    def solve(n, _):
        lanes = pl.ds(pl.multiple_of(n * 256, 256), 256)
        squares = jnp.zeros((1, 256), F32)
        for b in range(2):
            for m in range(2):
                rows8 = []
                for i in range(32):
                    at = i + late[m][b]
                    rows8.append(jnp.where(source[b], zst[m, at, :, lanes], zpt[m, at, :, lanes]))
                r = jnp.concatenate(rows8, axis=0)
                if b == 1:
                    r = r - dot3(
                        lh[2, m * 256 : m * 256 + 256, :], ll[2, m * 256 : m * 256 + 256, :],
                        xh_ref[0:512, lanes], xl_ref[0:512, lanes],
                    )
                if m == 1:
                    r = r - dot3(
                        lh[b, 256:512, 0:256], ll[b, 256:512, 0:256],
                        xh_ref[b * 512 : b * 512 + 256, lanes], xl_ref[b * 512 : b * 512 + 256, lanes],
                    )
                rh, rl = split(r)
                x = dot3(dh[b * 2 + m], dl[b * 2 + m], rh, rl)
                hi, lo = split(x)
                at = b * 512 + m * 256
                xh_ref[at : at + 256, lanes] = hi
                xl_ref[at : at + 256, lanes] = lo
                squares = squares + jnp.sum(x * x, axis=0, keepdims=True)
        varo_ref[:, lanes] = var_ref[:, lanes] - squares
        return 0

    lax.fori_loop(0, 4, solve, 0)


def update(info_ref, ph_ref, pl_ref, xh_ref, xl_ref, w_ref, o_ref):
    n = pl.program_id(0)
    block = (n // 2) * info_ref[2] + info_ref[1]
    j = info_ref[0]

    @pl.when(block > j + 1)
    def _():
        o_ref[...] = w_ref[...] - dot3(ph_ref[...], pl_ref[...], xh_ref[...], xl_ref[...])

    @pl.when(block < j)
    def _():
        o_ref[...] = w_ref[...]

    for k in range(2):

        @pl.when(block == j + k)
        def _():
            rows = pl.ds(pl.multiple_of(k * 512 + lax.rem(n, 2) * 256, 256), 256)
            o_ref[...] = xh_ref[rows, :].astype(F32) + xl_ref[rows, :].astype(F32)


def per_device(factor, pending, variance, first_block):
    f = factor.reshape(8192, 128)
    w = pending.reshape(1024, 1024)
    vmem = pl.BlockSpec(memory_space=pltpu.VMEM)
    smem = pl.BlockSpec(memory_space=pltpu.SMEM)
    dma = pltpu.SemaphoreType.DMA
    sd = jax.ShapeDtypeStruct
    xh, xl, ph, plo, var = pl.pallas_call(
        exchange,
        out_shape=[sd((1024, 1024), BF16)] * 4 + [sd((1, 1024), F32)],
        in_specs=[smem, smem, vmem, vmem, vmem],
        out_specs=[vmem] * 5,
        scratch_shapes=[
            pltpu.VMEM((4, SXY, 2, 8, 512), F32),
            pltpu.VMEM((4, SXY, 2, 8, 512), F32),
            pltpu.VMEM((2, SZ, 8, 1024), F32),
            pltpu.VMEM((2, ZSEND, 8, 1024), F32),
            pltpu.VMEM((2, SZ, 8, 1024), F32),
            pltpu.VMEM((16, 16, 8, 128), F32),
            pltpu.VMEM((16, 8, 128), F32),
            pltpu.VMEM((16, 8, 128), F32),
            pltpu.VMEM((16, 2, 8, 128), F32),
            pltpu.VMEM((16, 2, 8, 128), F32),
            pltpu.VMEM((2, 16, 8, 3, 8, 128), F32),
            pltpu.VMEM((3, 512, 512), BF16),
            pltpu.VMEM((3, 512, 512), BF16),
            pltpu.VMEM((4, 256, 256), BF16),
            pltpu.VMEM((4, 256, 256), BF16),
            dma((4,)), dma((4, SXY)), dma((2,)), dma((2, ZSEND)), dma((2,)), dma((2,)),
            dma, dma((2,)), dma, dma((16,)), dma, dma((16,)), dma, dma((16, 4)), dma, dma,
        ],
        compiler_params=pltpu.CompilerParams(
            collective_id=0, has_side_effects=True, vmem_limit_bytes=67043328
        ),
        name="exchange",
    )(first_block, jnp.asarray(tree_table()), f, w, variance.reshape(1, 1024))

    info = jnp.stack([first_block[0], lax.axis_index("row"), jnp.int32(16)]).astype(jnp.int32)
    full = pl.BlockSpec((1024, 1024), lambda n, info: (0, 0))
    part = pl.BlockSpec((256, 1024), lambda n, info: (n, 0))
    out = pl.pallas_call(
        update,
        out_shape=sd((1024, 1024), F32),
        grid_spec=pltpu.PrefetchScalarGridSpec(
            num_scalar_prefetch=1,
            grid=(4,),
            in_specs=[part, part, full, full, part],
            out_specs=part,
        ),
        compiler_params=pltpu.CompilerParams(vmem_limit_bytes=60 << 20),
        name="update",
    )(info, ph, plo, xh, xl, w)
    return out.reshape(pending.shape), var.reshape(1024)


def solution(mesh):
    in_specs = (P(None, "row", None, None, "col", None), P(None, "row", None, "col"), P("col"), P())
    out_specs = (P(None, "row", None, "col"), P("col"))
    return jax.shard_map(
        per_device, mesh=mesh, in_specs=in_specs, out_specs=out_specs, check_vma=False
    )
```

```python
import functools

import jax
import jax.numpy as jnp
import numpy as np
from jax import lax
from jax.experimental import pallas as pl
from jax.experimental.pallas import tpu as pltpu
from jax.sharding import PartitionSpec as P

MESH = pl.DeviceIdType.MESH
F32 = jnp.float32
BF16 = jnp.bfloat16

PI = [
    [-1, 0, 0, 0, 1, 2, 2, 0, 1, 2, 2, 0, 1, 3, 0, 0],
    [-1, 1, 1, 1, 0, 1, 1, 2, 0, 1, 3, 2, 0, 1, 3, 3],
    [-1, 3, 3, 3, 2, 0, 0, 1, 2, 0, 1, 1, 2, 2, 2, 2],
    [-1, 2, 2, 2, 3, 3, 3, 3, 3, 3, 0, 3, 3, 0, 1, 1],
]
K = [
    [0, 1, 2, 3, 3, 2, 3, 4, 4, 3, 4, 5, 3, 2, 3, 4],
    [0, 3, 2, 1, 3, 4, 3, 2, 4, 5, 4, 3, 3, 4, 3, 2],
    [0, 3, 4, 3, 1, 2, 3, 2, 2, 3, 4, 3, 3, 4, 5, 4],
    [0, 3, 4, 3, 3, 4, 5, 4, 2, 3, 4, 3, 1, 2, 3, 2],
]
STEP = [(1, 0), (3, 0), (0, 1), (0, 3)]
DEPTH = 5
D = 5
DZ = 5
NPZ = 32
SZ = NPZ + 7 * DZ
ZSEND = NPZ + 6 * DZ
EV_A2A, EV_SEL, EV_AG = 16, 23, 30
EV_STEP = 6


def hop(v, d):
    return ((v // 4 + STEP[d][1]) % 4) * 4 + (v % 4 + STEP[d][0]) % 4


def tree_table():
    rows = []
    for u in range(16):
        pick = []
        for d in range(4):
            v = hop(u, d)
            if u == 0 or v == 0:
                pick.append(4)
            else:
                c = [c for c in range(4) if PI[c][v] == d][0]
                pick.append(PI[c][u])
        rows.append(pick + [max(PI[c][u], 0) for c in range(4)] + [max(K[c][u] - 1, 0) * D for c in range(4)])
    return np.array(rows, np.int32).reshape(-1)


def iota2(n, dim):
    return lax.broadcasted_iota(jnp.int32, (n, n), dim)


def dot6(a, b):
    return jnp.dot(a, b, precision=lax.Precision.HIGHEST, preferred_element_type=F32)


def split(x):
    hi = x.astype(BF16)
    return hi, (x - hi.astype(F32)).astype(BF16)


def dot3(ah, al, bh, bl):
    f = functools.partial(jnp.dot, preferred_element_type=F32)
    return f(ah, bh) + (f(ah, bl) + f(al, bh))


def inverses(blocks):
    n = blocks[0].shape[0]
    r, c = iota2(n, 0), iota2(n, 1)
    eye = (r == c).astype(F32)
    scale = [1.0 / jnp.sum(jnp.where(r == c, b, 0.0), axis=1, keepdims=True) for b in blocks]
    scale_t = [1.0 / jnp.sum(jnp.where(r == c, b, 0.0), axis=0, keepdims=True) for b in blocks]
    strict = [jnp.where(r > c, b * s, 0.0) for b, s in zip(blocks, scale)]
    small = [jnp.where(r // 16 == c // 16, x, 0.0) for x in strict]
    inv = [eye - x for x in small]
    power = small
    for _ in range(3):
        power = [dot6(x, x) for x in power]
        inv = [dot6(e, eye + x) for e, x in zip(inv, power)]
    size = 16
    while size < n:
        off = [jnp.where((r // (2 * size) == c // (2 * size)) & (r // size != c // size), x, 0.0) for x in strict]
        mid = [dot6(f, e) for f, e in zip(off, inv)]
        inv = [e - dot6(e, m) for e, m in zip(inv, mid)]
        size *= 2
    return [e * s for e, s in zip(inv, scale_t)]


def exchange(
    base, first_ref, tbl_ref, f_ref, w_ref, var_ref,
    xh_ref, xl_ref, ph_ref, pl_ref, varo_ref,
    xst, xrc, zst, zrc, zpt, cand, ta, tb, tab, a2a, tg, lh, ll, dh, dl,
    xs, xr, zs, zr, zps, zpr, scs, scr, a2s, a2r, ags, agr, x2s, x2r, tps, tpr,
):
    tall = (1024 - base) // 4
    NPX = tall // 8
    SXY = NPX + (DEPTH - 1) * D
    groups = tall // 4
    each = -(-groups // (ZSEND - SXY - D))
    p = lax.axis_index("row")
    s = lax.axis_index("col")
    zc, core = p // 2, lax.rem(p, 2)
    yc, xc = s // 4, lax.rem(s, 4)
    partner = (p + 1 - 2 * core, s)
    near = [
        (p, yc * 4 + lax.rem(xc + 1, 4)),
        (p, yc * 4 + lax.rem(xc + 3, 4)),
        (p, lax.rem(yc + 1, 4) * 4 + xc),
        (p, lax.rem(yc + 3, 4) * 4 + xc),
    ]
    zup = (lax.rem(zc + 1, 8) * 2 + core, s)
    zdn = (lax.rem(zc + 7, 8) * 2 + core, s)
    znear = [zup, zdn]

    def rcopy(src, dst, ssem, rsem, dev):
        return pltpu.make_async_remote_copy(
            src_ref=src, dst_ref=dst, send_sem=ssem, recv_sem=rsem, device_id=dev, device_id_type=MESH
        )

    barrier = pltpu.get_barrier_semaphore()
    for o in range(1, 16):
        pl.semaphore_signal(barrier, inc=1, device_id=(p, lax.rem(s + o, 16)), device_id_type=MESH)
        pl.semaphore_signal(barrier, inc=1, device_id=(lax.rem(p + o, 16), s), device_id_type=MESH)

    j = first_ref[0]
    j1 = j + 1
    pj, pj1 = lax.rem(j, 16), lax.rem(j1, 16)
    c1, c2 = j // 16, j1 // 16
    crit = jnp.where(p == pj1, c2, c1)
    zroot = (p == pj) | (p == pj1)
    rel = []
    for root in (pj, pj1):
        ry, rx = root // 4, lax.rem(root, 4)
        rel.append((lax.rem(yc - ry + 4, 4) * 4 + lax.rem(xc - rx + 4, 4)) * 12)
    pick = [[tbl_ref[rel[q] + d] for d in range(4)] for q in range(2)]
    where_dir = [[tbl_ref[rel[q] + 4 + c] for c in range(4)] for q in range(2)]
    where_slot = [[tbl_ref[rel[q] + 8 + c] for c in range(4)] for q in range(2)]
    proot = [rel[0] == 0, rel[1] == 0]
    ccyc = jnp.where(proot[0], c1, c2)

    def panel(row, cyc_q, ct):
        low, high = (f_ref[pl.ds(row * 8 + c * 4 + ct, 8, stride=8), :] for c in range(2))
        return jnp.where(cyc_q == 0, low, high)

    def rhs(row):
        return jnp.where(crit == 0, w_ref[pl.ds(row, 8), :], w_ref[pl.ds(512 + row, 8), :])

    is_a = s == p
    is_b = s == lax.rem(p + 15, 16)
    cidx = jnp.where(is_a, crit, c1)

    @pl.when(is_a | is_b)
    def _():
        def fill(q, _):
            for u in range(16):
                low, high = (panel(a * 512 + q * 32 + (u // 4) * 8, cidx, u % 4) for a in range(2))
                cand[q, u] = jnp.where(crit == 0, low, high)
            return 0

        lax.fori_loop(0, 16, fill, 0)

    pl.semaphore_wait(barrier, 30)

    for flag, dest, k in ((is_a, ta, 0), (is_b, tb, 1)):

        @pl.when(flag)
        def _():
            for o in range(1, 16):
                to = lax.rem(s + o, 16)
                rcopy(cand.at[to], dest, scs, scr.at[k], (p, to)).start()

    def ev_a2a():
        for flag, dest, k in ((is_a, ta, 0), (is_b, tb, 1)):

            @pl.when(flag)
            def _():
                for u in range(16):
                    dest[u] = cand[s, u]

            @pl.when(jnp.logical_not(flag))
            def _():
                rcopy(cand.at[0], dest, scs, scr.at[k], partner).wait_recv()

        for u in range(16):
            tab[u, 0] = ta[u]
            tab[u, 1] = tb[u]
        a2a[p] = tab[p]
        for o in range(1, 16):
            to = lax.rem(p + o, 16)
            rcopy(tab.at[to], a2a.at[p], a2s, a2r.at[p], (to, s)).start()

    def ev_sel():
        for o in range(1, 16):
            frm = lax.rem(p + o, 16)
            rcopy(tab.at[0], a2a.at[frm], a2s, a2r.at[frm], partner).wait_recv()
        h, u = p // 8, lax.rem(p, 8)
        tg[h, s, u, 0] = a2a[pj, 0]
        tg[h, s, u, 1] = a2a[pj1, 0]
        tg[h, s, u, 2] = a2a[pj1, 1]
        for o in range(1, 16):
            to = lax.rem(p + o, 16)
            rcopy(tg.at[h, s, u], tg.at[h, s, u], ags, agr.at[p], (to, s)).start()

    def piece(root, c):
        return tg.at[core, root, pl.ds(2 * c, 2)]

    def ev_ag(k):
        if k == 0:
            for o in range(1, 16):
                frm = lax.rem(p + o, 16)
                rcopy(
                    tg.at[0, 0, 0], tg.at[frm // 8, s, lax.rem(frm, 8)], ags, agr.at[frm], partner
                ).wait_recv()
        for w in range(16):
            for c in range(4):
                if K[c][w] != k:
                    continue
                root = lax.rem(yc + 4 - w // 4, 4) * 4 + lax.rem(xc + 4 - w % 4, 4)
                if w:
                    rcopy(piece(root, c), piece(root, c), x2s, x2r.at[root, c], partner).wait_recv()
                    rcopy(piece(root, c), piece(root, c), tps, tpr, partner).start()
                for d in range(4):
                    v = hop(w, d)
                    if v and PI[c][v] == d and (w or d == c):
                        rcopy(piece(root, c), piece(root, c), x2s, x2r.at[root, c], near[d]).start()

    def panels(g):
        colour, i = g // (tall // 16), lax.rem(g, tall // 16) * 2
        row = pl.multiple_of(base + g * 16, 16)
        own = [[panel(row + e * 8, ccyc, ct) for ct in range(4)] for e in range(2)]
        for q in range(2):
            here, late = where_dir[q][0], where_slot[q][0]
            for c in range(1, 4):
                here = jnp.where(colour == c, where_dir[q][c], here)
                late = jnp.where(colour == c, where_slot[q][c], late)
            for ct in range(4):
                parts = []
                for e in range(2):
                    got = xrc[here, i + e + late, q, :, ct * 128 : ct * 128 + 128]
                    parts.append(jnp.where(proot[q], own[e][ct], got))
                hi, lo = split(jnp.concatenate(parts, axis=0))
                lanes = slice(q * 512 + ct * 128, q * 512 + ct * 128 + 128)
                ph_ref[pl.ds(row, 16), lanes] = hi
                pl_ref[pl.ds(row, 16), lanes] = lo

    def slot(t, _):
        back = t - D
        zback = t - DZ

        own_x = base + jnp.minimum(t, NPX - 1) * 8
        own_z = jnp.minimum(t, NPZ - 1) * 8

        @pl.when(t >= DZ)
        def _():
            for d in range(2):
                rcopy(zst.at[d, zback], zrc.at[d, zback], zs.at[d], zr.at[d, zback], znear[d]).wait_recv()

        @pl.when(t < DZ)
        def _():
            for d in range(2):
                zst[d, t] = rhs(pl.multiple_of(d * 256 + own_z, 8))

        @pl.when((t >= DZ) & (t < NPZ))
        def _():
            for d in range(2):
                own = rhs(pl.multiple_of(d * 256 + own_z, 8))
                zst[d, t] = jnp.where(zroot, own, zrc[d, zback])

        @pl.when(t >= NPZ)
        def _():
            for d in range(2):
                zst[d, t] = zrc[d, zback]

        @pl.when(t < ZSEND)
        def _():
            for d in range(2):
                rcopy(zst.at[d, t], zrc.at[d, t], zs.at[d], zr.at[d, t], znear[d]).start()

        for d in range(2):
            rcopy(zst.at[d, t], zpt.at[d, t], zps.at[d], zpr.at[d], partner).start()

        @pl.when((t >= D) & (back < SXY))
        def _():
            for d in range(4):
                rcopy(xst.at[d, back], xrc.at[d, back], xs.at[d], xr.at[d, back], near[d]).wait_recv()

        def put_xy(d):
            rcopy(xst.at[d, t], xrc.at[d, t], xs.at[d], xr.at[d, t], near[d]).start()

        @pl.when(t < D)
        def _():
            for d in range(4):
                for ct in range(4):
                    lanes = slice(ct * 128, ct * 128 + 128)
                    own = panel(d * tall + own_x, ccyc, ct)
                    for q in range(2):
                        xst[d, t, q, :, lanes] = own
                put_xy(d)

        @pl.when((t >= D) & (t < NPX))
        def _():
            for d in range(4):
                for ct in range(4):
                    lanes = slice(ct * 128, ct * 128 + 128)
                    own = panel(d * tall + own_x, ccyc, ct)
                    for q in range(2):
                        v = own
                        for e in range(4):
                            v = jnp.where(pick[q][d] == e, xrc[e, back, q, :, lanes], v)
                        xst[d, t, q, :, lanes] = v
                put_xy(d)

        @pl.when((t >= NPX) & (t < SXY))
        def _():
            for d in range(4):
                for q in range(2):
                    v = xrc[0, back, q]
                    for e in range(1, 4):
                        v = jnp.where(pick[q][d] == e, xrc[e, back, q], v)
                    xst[d, t, q] = v
                put_xy(d)

        @pl.when((t >= SXY + D) & (t < ZSEND))
        def _():
            def rows(n, _):
                panels(jnp.minimum((t - SXY - D) * each + n, groups - 1))
                return 0

            lax.fori_loop(0, each, rows, 0)

        pl.when(t == EV_A2A)(ev_a2a)
        pl.when(t == EV_SEL)(ev_sel)
        for k in range(DEPTH + 1):
            pl.when(t == EV_AG + k * EV_STEP)(functools.partial(ev_ag, k))
        return 0

    lax.fori_loop(0, ZSEND, slot, 0)

    half = tg.at[core, pl.ds(0, 15)]
    rcopy(half, half, tps, tpr, partner).wait()

    def tile(b, rt, ct):
        u = (rt % 4) * 4 + ct
        return tg[u // 8, rt // 4, u % 8, b]

    def triangle(q, _):
        for b in range(3):
            for pair in range(2):
                for ct in range(4):
                    u = pair * 8 + ct
                    x = jnp.concatenate([tg[u // 8, q, u % 8, b], tg[(u + 4) // 8, q, (u + 4) % 8, b]], axis=0)
                    hi, lo = split(x)
                    rows16 = pl.ds(pl.multiple_of(q * 32 + pair * 16, 16), 16)
                    lh[b, rows16, ct * 128 : ct * 128 + 128] = hi
                    ll[b, rows16, ct * 128 : ct * 128 + 128] = lo
        return 0

    lax.fori_loop(0, 16, triangle, 0)

    def square(b, m, k):
        return jnp.concatenate(
            [
                jnp.concatenate([tile(b, m * 16 + rt, k * 1 + ct) for ct in range(1)], axis=1)
                for rt in range(16)
            ],
            axis=0,
        )

    inv = inverses([square(b, m, m) for b in range(2) for m in range(4)])
    for b in range(2):
        for m in range(2):
            top, bottom = inv[b * 4 + 2 * m], inv[b * 4 + 2 * m + 1]
            corner = -dot6(bottom, dot6(square(b, 2 * m + 1, 2 * m), top))
            for (r0, c0), x in (((0, 0), top), ((1, 1), bottom), ((1, 0), corner), ((0, 1), jnp.zeros_like(top))):
                hi, lo = split(x)
                dh[b * 2 + m, r0 * 128 : r0 * 128 + 128, c0 * 128 : c0 * 128 + 128] = hi
                dl[b * 2 + m, r0 * 128 : r0 * 128 + 128, c0 * 128 : c0 * 128 + 128] = lo

    lax.fori_loop(ZSEND, SZ, slot, 0)

    for d in range(4):
        rcopy(xst.at[d], xrc.at[d], xs.at[d], xr.at[d, 0], partner).wait_send()
    for d in range(2):
        rcopy(zrc.at[d], zrc.at[d], zs.at[d], zr.at[d, 0], partner).wait_send()
        rcopy(zst.at[d], zpt.at[d], zps.at[d], zpr.at[d], partner).wait()
    rcopy(half, half, x2s, tpr, partner).wait_send()
    rcopy(a2a.at[pl.ds(0, 15)], a2a.at[pl.ds(0, 15)], a2s, tpr, partner).wait_send()
    rcopy(tg.at[0, pl.ds(0, 15), 0], tg.at[0, pl.ds(0, 15), 0], ags, tpr, partner).wait_send()

    @pl.when(is_a | is_b)
    def _():
        rcopy(cand.at[pl.ds(0, 15)], cand.at[pl.ds(0, 15)], scs, tpr, partner).wait_send()

    zroots = [pj // 2, pj1 // 2]
    source = [lax.rem(pj, 2) == core, lax.rem(pj1, 2) == core]
    late = [
        [lax.rem(zc - z + 8, 8) * DZ for z in zroots],
        [lax.rem(z - zc + 8, 8) * DZ for z in zroots],
    ]

    def solve(n, _):
        lanes = pl.ds(pl.multiple_of(n * 256, 256), 256)
        squares = jnp.zeros((1, 256), F32)
        for b in range(2):
            for m in range(2):
                rows8 = []
                for i in range(32):
                    at = i + late[m][b]
                    rows8.append(jnp.where(source[b], zst[m, at, :, lanes], zpt[m, at, :, lanes]))
                r = jnp.concatenate(rows8, axis=0)
                if b == 1:
                    r = r - dot3(
                        lh[2, m * 256 : m * 256 + 256, :], ll[2, m * 256 : m * 256 + 256, :],
                        xh_ref[0:512, lanes], xl_ref[0:512, lanes],
                    )
                if m == 1:
                    r = r - dot3(
                        lh[b, 256:512, 0:256], ll[b, 256:512, 0:256],
                        xh_ref[b * 512 : b * 512 + 256, lanes], xl_ref[b * 512 : b * 512 + 256, lanes],
                    )
                rh, rl = split(r)
                x = dot3(dh[b * 2 + m], dl[b * 2 + m], rh, rl)
                hi, lo = split(x)
                at = b * 512 + m * 256
                xh_ref[at : at + 256, lanes] = hi
                xl_ref[at : at + 256, lanes] = lo
                squares = squares + jnp.sum(x * x, axis=0, keepdims=True)
        varo_ref[:, lanes] = var_ref[:, lanes] - squares
        return 0

    lax.fori_loop(0, 4, solve, 0)


def update(info_ref, ph_ref, pl_ref, xh_ref, xl_ref, w_ref, o_ref):
    n = pl.program_id(0)
    block = (n // 2) * info_ref[2] + info_ref[1]
    j = info_ref[0]

    @pl.when(block > j + 1)
    def _():
        o_ref[...] = w_ref[...] - dot3(ph_ref[...], pl_ref[...], xh_ref[...], xl_ref[...])

    @pl.when(block < j)
    def _():
        o_ref[...] = w_ref[...]

    for k in range(2):

        @pl.when(block == j + k)
        def _():
            rows = pl.ds(pl.multiple_of(k * 512 + lax.rem(n, 2) * 256, 256), 256)
            o_ref[...] = xh_ref[rows, :].astype(F32) + xl_ref[rows, :].astype(F32)


def per_device(factor, pending, variance, first_block):
    f = factor.reshape(8192, 128)
    w = pending.reshape(1024, 1024)
    vmem = pl.BlockSpec(memory_space=pltpu.VMEM)
    smem = pl.BlockSpec(memory_space=pltpu.SMEM)
    dma = pltpu.SemaphoreType.DMA
    sd = jax.ShapeDtypeStruct
    def moved(base, *operands):
        sxy = (1024 - base) // 32 + (DEPTH - 1) * D
        return pl.pallas_call(
            functools.partial(exchange, base),
            out_shape=[sd((1024, 1024), BF16)] * 4 + [sd((1, 1024), F32)],
            in_specs=[smem, smem, vmem, vmem, vmem],
            out_specs=[vmem] * 5,
            scratch_shapes=[
                pltpu.VMEM((4, sxy, 2, 8, 512), F32),
                pltpu.VMEM((4, sxy, 2, 8, 512), F32),
                pltpu.VMEM((2, SZ, 8, 1024), F32),
                pltpu.VMEM((2, ZSEND, 8, 1024), F32),
                pltpu.VMEM((2, SZ, 8, 1024), F32),
                pltpu.VMEM((16, 16, 8, 128), F32),
                pltpu.VMEM((16, 8, 128), F32),
                pltpu.VMEM((16, 8, 128), F32),
                pltpu.VMEM((16, 2, 8, 128), F32),
                pltpu.VMEM((16, 2, 8, 128), F32),
                pltpu.VMEM((2, 16, 8, 3, 8, 128), F32),
                pltpu.VMEM((3, 512, 512), BF16),
                pltpu.VMEM((3, 512, 512), BF16),
                pltpu.VMEM((4, 256, 256), BF16),
                pltpu.VMEM((4, 256, 256), BF16),
                dma((4,)), dma((4, sxy)), dma((2,)), dma((2, ZSEND)), dma((2,)), dma((2,)),
                dma, dma((2,)), dma, dma((16,)), dma, dma((16,)), dma, dma((16, 4)), dma, dma,
            ],
            compiler_params=pltpu.CompilerParams(
                collective_id=base // 512, has_side_effects=True, vmem_limit_bytes=67043328
            ),
            name="exchange" + str(base),
        )(*operands)

    xh, xl, ph, plo, var = lax.cond(
        first_block[0] >= 15,
        functools.partial(moved, 512),
        functools.partial(moved, 0),
        first_block, jnp.asarray(tree_table()), f, w, variance.reshape(1, 1024),
    )

    info = jnp.stack([first_block[0], lax.axis_index("row"), jnp.int32(16)]).astype(jnp.int32)
    full = pl.BlockSpec((1024, 1024), lambda n, info: (0, 0))
    part = pl.BlockSpec((256, 1024), lambda n, info: (n, 0))
    out = pl.pallas_call(
        update,
        out_shape=sd((1024, 1024), F32),
        grid_spec=pltpu.PrefetchScalarGridSpec(
            num_scalar_prefetch=1,
            grid=(4,),
            in_specs=[part, part, full, full, part],
            out_specs=part,
        ),
        compiler_params=pltpu.CompilerParams(vmem_limit_bytes=60 << 20),
        name="update",
    )(info, ph, plo, xh, xl, w)
    return out.reshape(pending.shape), var.reshape(1024)


def solution(mesh):
    in_specs = (P(None, "row", None, None, "col", None), P(None, "row", None, "col"), P("col"), P())
    out_specs = (P(None, "row", None, "col"), P("col"))
    return jax.shard_map(
        per_device, mesh=mesh, in_specs=in_specs, out_specs=out_specs, check_vma=False
    )
```

```python
import functools

import jax
import jax.numpy as jnp
import numpy as np
from jax import lax
from jax.experimental import pallas as pl
from jax.experimental.pallas import tpu as pltpu
from jax.sharding import PartitionSpec as P

MESH = pl.DeviceIdType.MESH
F32 = jnp.float32
BF16 = jnp.bfloat16

PI = [
    [-1, 0, 0, 0, 1, 2, 2, 0, 1, 2, 2, 0, 1, 3, 0, 0],
    [-1, 1, 1, 1, 0, 1, 1, 2, 0, 1, 3, 2, 0, 1, 3, 3],
    [-1, 3, 3, 3, 2, 0, 0, 1, 2, 0, 1, 1, 2, 2, 2, 2],
    [-1, 2, 2, 2, 3, 3, 3, 3, 3, 3, 0, 3, 3, 0, 1, 1],
]
K = [
    [0, 1, 2, 3, 3, 2, 3, 4, 4, 3, 4, 5, 3, 2, 3, 4],
    [0, 3, 2, 1, 3, 4, 3, 2, 4, 5, 4, 3, 3, 4, 3, 2],
    [0, 3, 4, 3, 1, 2, 3, 2, 2, 3, 4, 3, 3, 4, 5, 4],
    [0, 3, 4, 3, 3, 4, 5, 4, 2, 3, 4, 3, 1, 2, 3, 2],
]
STEP = [(1, 0), (3, 0), (0, 1), (0, 3)]
DEPTH = 5
D = 5
DZ = 5
NPZ = 32
SZ = NPZ + 7 * DZ
ZSEND = NPZ + 6 * DZ
EV_A2A, EV_SEL, EV_AG = 16, 23, 30
EV_STEP = 6


def hop(v, d):
    return ((v // 4 + STEP[d][1]) % 4) * 4 + (v % 4 + STEP[d][0]) % 4


def tree_table():
    rows = []
    for u in range(16):
        pick = []
        for d in range(4):
            v = hop(u, d)
            if u == 0 or v == 0:
                pick.append(4)
            else:
                c = [c for c in range(4) if PI[c][v] == d][0]
                pick.append(PI[c][u])
        rows.append(pick + [max(PI[c][u], 0) for c in range(4)] + [max(K[c][u] - 1, 0) * D for c in range(4)])
    return np.array(rows, np.int32).reshape(-1)


def iota2(n, dim):
    return lax.broadcasted_iota(jnp.int32, (n, n), dim)


def dot6(a, b):
    return jnp.dot(a, b, precision=lax.Precision.HIGHEST, preferred_element_type=F32)


def split(x):
    hi = x.astype(BF16)
    return hi, (x - hi.astype(F32)).astype(BF16)


def dot3(ah, al, bh, bl):
    f = functools.partial(jnp.dot, preferred_element_type=F32)
    return f(ah, bh) + (f(ah, bl) + f(al, bh))


def inverses(blocks):
    n = blocks[0].shape[0]
    r, c = iota2(n, 0), iota2(n, 1)
    eye = (r == c).astype(F32)
    scale = [1.0 / jnp.sum(jnp.where(r == c, b, 0.0), axis=1, keepdims=True) for b in blocks]
    scale_t = [1.0 / jnp.sum(jnp.where(r == c, b, 0.0), axis=0, keepdims=True) for b in blocks]
    strict = [jnp.where(r > c, b * s, 0.0) for b, s in zip(blocks, scale)]
    small = [jnp.where(r // 16 == c // 16, x, 0.0) for x in strict]
    inv = [eye - x for x in small]
    power = small
    for _ in range(3):
        power = [dot6(x, x) for x in power]
        inv = [dot6(e, eye + x) for e, x in zip(inv, power)]
    size = 16
    while size < n:
        off = [jnp.where((r // (2 * size) == c // (2 * size)) & (r // size != c // size), x, 0.0) for x in strict]
        mid = [dot6(f, e) for f, e in zip(off, inv)]
        inv = [e - dot6(e, m) for e, m in zip(inv, mid)]
        size *= 2
    return [e * s for e, s in zip(inv, scale_t)]


def exchange(
    base, first_ref, tbl_ref, f_ref, w_ref, var_ref,
    xh_ref, xl_ref, ph_ref, pl_ref, varo_ref,
    xst, xrc, zst, zrc, zpt, cand, ta, tb, tab, a2a, tg, lh, ll, dh, dl,
    xs, xr, zs, zr, zps, zpr, scs, scr, a2s, a2r, ags, agr, x2s, x2r, tps, tpr,
):
    tall = (1024 - base) // 4
    NPX = tall // 8
    SXY = NPX + (DEPTH - 1) * D
    groups = tall // 4
    each = -(-groups // (ZSEND - SXY - D))
    p = lax.axis_index("row")
    s = lax.axis_index("col")
    zc, core = p // 2, lax.rem(p, 2)
    yc, xc = s // 4, lax.rem(s, 4)
    partner = (p + 1 - 2 * core, s)
    near = [
        (p, yc * 4 + lax.rem(xc + 1, 4)),
        (p, yc * 4 + lax.rem(xc + 3, 4)),
        (p, lax.rem(yc + 1, 4) * 4 + xc),
        (p, lax.rem(yc + 3, 4) * 4 + xc),
    ]
    zup = (lax.rem(zc + 1, 8) * 2 + core, s)
    zdn = (lax.rem(zc + 7, 8) * 2 + core, s)
    znear = [zup, zdn]

    def rcopy(src, dst, ssem, rsem, dev):
        return pltpu.make_async_remote_copy(
            src_ref=src, dst_ref=dst, send_sem=ssem, recv_sem=rsem, device_id=dev, device_id_type=MESH
        )

    barrier = pltpu.get_barrier_semaphore()
    for o in range(1, 16):
        pl.semaphore_signal(barrier, inc=1, device_id=(p, lax.rem(s + o, 16)), device_id_type=MESH)
        pl.semaphore_signal(barrier, inc=1, device_id=(lax.rem(p + o, 16), s), device_id_type=MESH)

    j = first_ref[0]
    j1 = j + 1
    pj, pj1 = lax.rem(j, 16), lax.rem(j1, 16)
    c1, c2 = j // 16, j1 // 16
    crit = jnp.where(p == pj1, c2, c1)
    zroot = (p == pj) | (p == pj1)
    rel = []
    for root in (pj, pj1):
        ry, rx = root // 4, lax.rem(root, 4)
        rel.append((lax.rem(yc - ry + 4, 4) * 4 + lax.rem(xc - rx + 4, 4)) * 12)
    pick = [[tbl_ref[rel[q] + d] for d in range(4)] for q in range(2)]
    where_dir = [[tbl_ref[rel[q] + 4 + c] for c in range(4)] for q in range(2)]
    where_slot = [[tbl_ref[rel[q] + 8 + c] for c in range(4)] for q in range(2)]
    proot = [rel[0] == 0, rel[1] == 0]
    ccyc = jnp.where(proot[0], c1, c2)

    def panel(row, cyc_q, ct):
        low, high = (f_ref[pl.ds(row * 8 + c * 4 + ct, 8, stride=8), :] for c in range(2))
        return jnp.where(cyc_q == 0, low, high)

    def rhs(row):
        return jnp.where(crit == 0, w_ref[pl.ds(row, 8), :], w_ref[pl.ds(512 + row, 8), :])

    is_a = s == p
    is_b = s == lax.rem(p + 15, 16)
    cidx = jnp.where(is_a, crit, c1)

    @pl.when(is_a | is_b)
    def _():
        def fill(q, _):
            for u in range(16):
                low, high = (panel(a * 512 + q * 32 + (u // 4) * 8, cidx, u % 4) for a in range(2))
                cand[q, u] = jnp.where(crit == 0, low, high)
            return 0

        lax.fori_loop(0, 16, fill, 0)

    pl.semaphore_wait(barrier, 30)

    for flag, dest, k in ((is_a, ta, 0), (is_b, tb, 1)):

        @pl.when(flag)
        def _():
            for o in range(1, 16):
                to = lax.rem(s + o, 16)
                rcopy(cand.at[to], dest, scs, scr.at[k], (p, to)).start()

    def ev_a2a():
        for flag, dest, k in ((is_a, ta, 0), (is_b, tb, 1)):

            @pl.when(flag)
            def _():
                for u in range(16):
                    dest[u] = cand[s, u]

            @pl.when(jnp.logical_not(flag))
            def _():
                rcopy(cand.at[0], dest, scs, scr.at[k], partner).wait_recv()

        for u in range(16):
            tab[u, 0] = ta[u]
            tab[u, 1] = tb[u]
        a2a[p] = tab[p]
        for o in range(1, 16):
            to = lax.rem(p + o, 16)
            rcopy(tab.at[to], a2a.at[p], a2s, a2r.at[p], (to, s)).start()

    def ev_sel():
        for o in range(1, 16):
            frm = lax.rem(p + o, 16)
            rcopy(tab.at[0], a2a.at[frm], a2s, a2r.at[frm], partner).wait_recv()
        h, u = p // 8, lax.rem(p, 8)
        tg[h, s, u, 0] = a2a[pj, 0]
        tg[h, s, u, 1] = a2a[pj1, 0]
        tg[h, s, u, 2] = a2a[pj1, 1]
        for o in range(1, 16):
            to = lax.rem(p + o, 16)
            rcopy(tg.at[h, s, u], tg.at[h, s, u], ags, agr.at[p], (to, s)).start()

    def piece(root, c):
        return tg.at[core, root, pl.ds(2 * c, 2)]

    def ev_ag(k):
        if k == 0:
            for o in range(1, 16):
                frm = lax.rem(p + o, 16)
                rcopy(
                    tg.at[0, 0, 0], tg.at[frm // 8, s, lax.rem(frm, 8)], ags, agr.at[frm], partner
                ).wait_recv()
        for w in range(16):
            for c in range(4):
                if K[c][w] != k:
                    continue
                root = lax.rem(yc + 4 - w // 4, 4) * 4 + lax.rem(xc + 4 - w % 4, 4)
                if w:
                    rcopy(piece(root, c), piece(root, c), x2s, x2r.at[root, c], partner).wait_recv()
                    rcopy(piece(root, c), piece(root, c), tps, tpr, partner).start()
                for d in range(4):
                    v = hop(w, d)
                    if v and PI[c][v] == d and (w or d == c):
                        rcopy(piece(root, c), piece(root, c), x2s, x2r.at[root, c], near[d]).start()

    def panels(g):
        colour, i = g // (tall // 16), lax.rem(g, tall // 16) * 2
        row = pl.multiple_of(base + g * 16, 16)
        own = [[panel(row + e * 8, ccyc, ct) for ct in range(4)] for e in range(2)]
        for q in range(2):
            here, late = where_dir[q][0], where_slot[q][0]
            for c in range(1, 4):
                here = jnp.where(colour == c, where_dir[q][c], here)
                late = jnp.where(colour == c, where_slot[q][c], late)
            for ct in range(4):
                parts = []
                for e in range(2):
                    got = xrc[here, i + e + late, q, :, ct * 128 : ct * 128 + 128]
                    parts.append(jnp.where(proot[q], own[e][ct], got))
                hi, lo = split(jnp.concatenate(parts, axis=0))
                lanes = slice(q * 512 + ct * 128, q * 512 + ct * 128 + 128)
                ph_ref[pl.ds(row, 16), lanes] = hi
                pl_ref[pl.ds(row, 16), lanes] = lo

    def slot(t, _):
        back = t - D
        zback = t - DZ

        own_x = base + jnp.minimum(t, NPX - 1) * 8
        own_z = jnp.minimum(t, NPZ - 1) * 8

        @pl.when(t >= DZ)
        def _():
            for d in range(2):
                rcopy(zst.at[d, zback], zrc.at[d, zback], zs.at[d], zr.at[d, zback], znear[d]).wait_recv()

        @pl.when(t < DZ)
        def _():
            for d in range(2):
                zst[d, t] = rhs(pl.multiple_of(d * 256 + own_z, 8))

        @pl.when((t >= DZ) & (t < NPZ))
        def _():
            for d in range(2):
                own = rhs(pl.multiple_of(d * 256 + own_z, 8))
                zst[d, t] = jnp.where(zroot, own, zrc[d, zback])

        @pl.when(t >= NPZ)
        def _():
            for d in range(2):
                zst[d, t] = zrc[d, zback]

        @pl.when(t < ZSEND)
        def _():
            for d in range(2):
                rcopy(zst.at[d, t], zrc.at[d, t], zs.at[d], zr.at[d, t], znear[d]).start()

        for d in range(2):
            rcopy(zst.at[d, t], zpt.at[d, t], zps.at[d], zpr.at[d], partner).start()

        @pl.when((t >= D) & (back < SXY))
        def _():
            for d in range(4):
                rcopy(xst.at[d, back], xrc.at[d, back], xs.at[d], xr.at[d, back], near[d]).wait_recv()

        def put_xy(d):
            rcopy(xst.at[d, t], xrc.at[d, t], xs.at[d], xr.at[d, t], near[d]).start()

        @pl.when(t < D)
        def _():
            for d in range(4):
                for ct in range(4):
                    lanes = slice(ct * 128, ct * 128 + 128)
                    own = panel(d * tall + own_x, ccyc, ct)
                    for q in range(2):
                        xst[d, t, q, :, lanes] = own
                put_xy(d)

        @pl.when((t >= D) & (t < NPX))
        def _():
            for d in range(4):
                for ct in range(4):
                    lanes = slice(ct * 128, ct * 128 + 128)
                    own = panel(d * tall + own_x, ccyc, ct)
                    for q in range(2):
                        v = own
                        for e in range(4):
                            v = jnp.where(pick[q][d] == e, xrc[e, back, q, :, lanes], v)
                        xst[d, t, q, :, lanes] = v
                put_xy(d)

        @pl.when((t >= NPX) & (t < SXY))
        def _():
            for d in range(4):
                for q in range(2):
                    v = xrc[0, back, q]
                    for e in range(1, 4):
                        v = jnp.where(pick[q][d] == e, xrc[e, back, q], v)
                    xst[d, t, q] = v
                put_xy(d)

        @pl.when((t >= SXY + D) & (t < ZSEND))
        def _():
            def rows(n, _):
                panels(jnp.minimum((t - SXY - D) * each + n, groups - 1))
                return 0

            lax.fori_loop(0, each, rows, 0)

        pl.when(t == EV_A2A)(ev_a2a)
        pl.when(t == EV_SEL)(ev_sel)
        for k in range(DEPTH + 1):
            pl.when(t == EV_AG + k * EV_STEP)(functools.partial(ev_ag, k))
        return 0

    lax.fori_loop(0, ZSEND, slot, 0)

    half = tg.at[core, pl.ds(0, 15)]
    rcopy(half, half, tps, tpr, partner).wait()

    def tile(b, rt, ct):
        u = (rt % 4) * 4 + ct
        return tg[u // 8, rt // 4, u % 8, b]

    def triangle(q, _):
        for b in range(3):
            for pair in range(2):
                for ct in range(4):
                    u = pair * 8 + ct
                    x = jnp.concatenate([tg[u // 8, q, u % 8, b], tg[(u + 4) // 8, q, (u + 4) % 8, b]], axis=0)
                    hi, lo = split(x)
                    rows16 = pl.ds(pl.multiple_of(q * 32 + pair * 16, 16), 16)
                    lh[b, rows16, ct * 128 : ct * 128 + 128] = hi
                    ll[b, rows16, ct * 128 : ct * 128 + 128] = lo
        return 0

    lax.fori_loop(0, 16, triangle, 0)

    def square(b, m, k):
        return jnp.concatenate(
            [
                jnp.concatenate([tile(b, m * 16 + rt, k * 1 + ct) for ct in range(1)], axis=1)
                for rt in range(16)
            ],
            axis=0,
        )

    inv = inverses([square(b, m, m) for b in range(2) for m in range(4)])
    for b in range(2):
        for m in range(2):
            top, bottom = inv[b * 4 + 2 * m], inv[b * 4 + 2 * m + 1]
            corner = -dot6(bottom, dot6(square(b, 2 * m + 1, 2 * m), top))
            for (r0, c0), x in (((0, 0), top), ((1, 1), bottom), ((1, 0), corner), ((0, 1), jnp.zeros_like(top))):
                hi, lo = split(x)
                dh[b * 2 + m, r0 * 128 : r0 * 128 + 128, c0 * 128 : c0 * 128 + 128] = hi
                dl[b * 2 + m, r0 * 128 : r0 * 128 + 128, c0 * 128 : c0 * 128 + 128] = lo

    lax.fori_loop(ZSEND, SZ, slot, 0)

    for d in range(4):
        rcopy(xst.at[d], xrc.at[d], xs.at[d], xr.at[d, 0], partner).wait_send()
    for d in range(2):
        rcopy(zrc.at[d], zrc.at[d], zs.at[d], zr.at[d, 0], partner).wait_send()
        rcopy(zst.at[d], zpt.at[d], zps.at[d], zpr.at[d], partner).wait()
    rcopy(half, half, x2s, tpr, partner).wait_send()
    rcopy(a2a.at[pl.ds(0, 15)], a2a.at[pl.ds(0, 15)], a2s, tpr, partner).wait_send()
    rcopy(tg.at[0, pl.ds(0, 15), 0], tg.at[0, pl.ds(0, 15), 0], ags, tpr, partner).wait_send()

    @pl.when(is_a | is_b)
    def _():
        rcopy(cand.at[pl.ds(0, 15)], cand.at[pl.ds(0, 15)], scs, tpr, partner).wait_send()

    zroots = [pj // 2, pj1 // 2]
    source = [lax.rem(pj, 2) == core, lax.rem(pj1, 2) == core]
    late = [
        [lax.rem(zc - z + 8, 8) * DZ for z in zroots],
        [lax.rem(z - zc + 8, 8) * DZ for z in zroots],
    ]

    def solve(n, _):
        lanes = pl.ds(pl.multiple_of(n * 256, 256), 256)
        squares = jnp.zeros((1, 256), F32)
        for b in range(2):
            for m in range(2):
                rows8 = []
                for i in range(32):
                    at = i + late[m][b]
                    rows8.append(jnp.where(source[b], zst[m, at, :, lanes], zpt[m, at, :, lanes]))
                r = jnp.concatenate(rows8, axis=0)
                if b == 1:
                    r = r - dot3(
                        lh[2, m * 256 : m * 256 + 256, :], ll[2, m * 256 : m * 256 + 256, :],
                        xh_ref[0:512, lanes], xl_ref[0:512, lanes],
                    )
                if m == 1:
                    r = r - dot3(
                        lh[b, 256:512, 0:256], ll[b, 256:512, 0:256],
                        xh_ref[b * 512 : b * 512 + 256, lanes], xl_ref[b * 512 : b * 512 + 256, lanes],
                    )
                rh, rl = split(r)
                x = dot3(dh[b * 2 + m], dl[b * 2 + m], rh, rl)
                hi, lo = split(x)
                at = b * 512 + m * 256
                xh_ref[at : at + 256, lanes] = hi
                xl_ref[at : at + 256, lanes] = lo
                squares = squares + jnp.sum(x * x, axis=0, keepdims=True)
        varo_ref[:, lanes] = var_ref[:, lanes] - squares
        return 0

    lax.fori_loop(0, 4, solve, 0)


def update(info_ref, ph_ref, pl_ref, xh_ref, xl_ref, w_ref, o_ref):
    n = pl.program_id(0)
    block = (n // 2) * info_ref[2] + info_ref[1]
    j = info_ref[0]

    @pl.when(block > j + 1)
    def _():
        here = pl.ds(pl.multiple_of(n * 256, 256), 256)
        o_ref[...] = w_ref[...] - dot3(ph_ref[here, :], pl_ref[here, :], xh_ref[...], xl_ref[...])

    @pl.when(block < j)
    def _():
        o_ref[...] = w_ref[...]

    for k in range(2):

        @pl.when(block == j + k)
        def _():
            rows = pl.ds(pl.multiple_of(k * 512 + lax.rem(n, 2) * 256, 256), 256)
            o_ref[...] = xh_ref[rows, :].astype(F32) + xl_ref[rows, :].astype(F32)


def per_device(factor, pending, variance, first_block):
    f = factor.reshape(8192, 128)
    w = pending.reshape(1024, 1024)
    vmem = pl.BlockSpec(memory_space=pltpu.VMEM)
    smem = pl.BlockSpec(memory_space=pltpu.SMEM)
    dma = pltpu.SemaphoreType.DMA
    sd = jax.ShapeDtypeStruct
    def moved(base, *operands):
        sxy = (1024 - base) // 32 + (DEPTH - 1) * D
        return pl.pallas_call(
            functools.partial(exchange, base),
            out_shape=[pltpu.VMEM((1024, 1024), BF16)] * 4 + [sd((1, 1024), F32)],
            in_specs=[smem, smem, vmem, vmem, vmem],
            out_specs=[vmem] * 5,
            scratch_shapes=[
                pltpu.VMEM((4, sxy, 2, 8, 512), F32),
                pltpu.VMEM((4, sxy, 2, 8, 512), F32),
                pltpu.VMEM((2, SZ, 8, 1024), F32),
                pltpu.VMEM((2, ZSEND, 8, 1024), F32),
                pltpu.VMEM((2, SZ, 8, 1024), F32),
                pltpu.VMEM((16, 16, 8, 128), F32),
                pltpu.VMEM((16, 8, 128), F32),
                pltpu.VMEM((16, 8, 128), F32),
                pltpu.VMEM((16, 2, 8, 128), F32),
                pltpu.VMEM((16, 2, 8, 128), F32),
                pltpu.VMEM((2, 16, 8, 3, 8, 128), F32),
                pltpu.VMEM((3, 512, 512), BF16),
                pltpu.VMEM((3, 512, 512), BF16),
                pltpu.VMEM((4, 256, 256), BF16),
                pltpu.VMEM((4, 256, 256), BF16),
                dma((4,)), dma((4, sxy)), dma((2,)), dma((2, ZSEND)), dma((2,)), dma((2,)),
                dma, dma((2,)), dma, dma((16,)), dma, dma((16,)), dma, dma((16, 4)), dma, dma,
            ],
            compiler_params=pltpu.CompilerParams(
                collective_id=base // 512, has_side_effects=True, vmem_limit_bytes=48 << 20
            ),
            name="exchange" + str(base),
        )(*operands)

    xh, xl, ph, plo, var = lax.cond(
        first_block[0] >= 15,
        functools.partial(moved, 512),
        functools.partial(moved, 0),
        first_block, jnp.asarray(tree_table()), f, w, variance.reshape(1, 1024),
    )

    info = jnp.stack([first_block[0], lax.axis_index("row"), jnp.int32(16)]).astype(jnp.int32)
    full = pl.BlockSpec(memory_space=pltpu.VMEM)
    part = pl.BlockSpec((256, 1024), lambda n, info: (n, 0))
    out = pl.pallas_call(
        update,
        out_shape=sd((1024, 1024), F32),
        grid_spec=pltpu.PrefetchScalarGridSpec(
            num_scalar_prefetch=1,
            grid=(4,),
            in_specs=[full] * 4 + [part],
            out_specs=part,
        ),
        compiler_params=pltpu.CompilerParams(vmem_limit_bytes=14 << 20),
        name="update",
    )(info, ph, plo, xh, xl, w)
    return out.reshape(pending.shape), var.reshape(1024)


def solution(mesh):
    in_specs = (P(None, "row", None, None, "col", None), P(None, "row", None, "col"), P("col"), P())
    out_specs = (P(None, "row", None, "col"), P("col"))
    return jax.shard_map(
        per_device, mesh=mesh, in_specs=in_specs, out_specs=out_specs, check_vma=False
    )
```
